32 devices in a mesh: comp: 2 (over core), tile: 16 (over z, y, x).
Axes of the slice: x: 2, y: 2, z: 4, core: 2. Of those that a mesh axis runs over, the one named last changes fastest.
Arguments:
- tracer: float32 [2, 16, 4, 64, 1024], P('comp', None, None, 'tile'), may hold values from -6 to 6
- velocity: float32 [2, 2, 4, 64, 1024], P('comp', None, None, 'tile'), may hold values from -0.3 to 0.3
- coupling: float32 [2, 16, 64, 1024], P('comp', None, 'tile'), may hold values from 0.05 to 0.5
- sea_mask: int32 [2, 64, 1024], P('comp', 'tile'), may hold values 0 or 1
- send_rows: int32 [2, 16, 4, 2048], P('comp', 'tile'), may hold values from 0 to 3
- send_cols: int32 [2, 16, 4, 2048], P('comp', 'tile'), may hold values from 0 to 1023
- intersection_near: int32 [2, 8, 64, 1024], P('comp', None, 'tile'), may hold values from 0 to 3
- intersection_slot: int32 [2, 8, 64, 1024], P('comp', None, 'tile'), may hold values from 0 to 2047
- intersection_weight: float32 [2, 8, 64, 1024], P('comp', None, 'tile'), as said below
Outputs:
- tracer_out: float32 [2, 16, 4, 64, 1024], P('comp', None, None, 'tile')
The draws below stay inside these ranges and needn't reach their ends.
Inputs may be any that keep to these rules, and one draw needn't show every extreme that they name: `intersection_weight`: positive, summing to one over the 8 intersections of a cell.
All inputs are finite; a program needn't handle non-finite values. No bound on the sum of `sea_mask` on one device may be relied on, other than what follows from the above.
Results may differ from the reference program's by a relative error of at most 0.000088.
Values sent between devices are 32-bit elements; how exact they have to be, the bound alone decides.
A program may use at most 64 MiB of HBM per device.

```python
import math
import jax
import jax.numpy as jnp
from jax import lax

CX = 4
NY = 1024
TRC = 16
LEV = 4
K = 8
NB = 4
CAP = 2048
NX = 64
N_TILE = 16


def draw_intersection_weight(key, part):
    raw = jax.random.uniform(key, (2, K, NX, NY), jnp.float32, 0.2, 1.0)
    return raw / jnp.sum(raw, axis=1, keepdims=True)


def with_ends(array, stream_key, low, high):
    extent = array.shape
    index_at = [jax.random.randint(jax.random.fold_in(stream_key, axis), (), 0, extent[axis]) for axis in range(len(extent))]
    array = array.at[tuple(index_at)].set(low)
    longest = extent.index(max(extent))
    index_at[longest] = (index_at[longest] + 1) % extent[longest]
    return array.at[tuple(index_at)].set(high)


def level_of(key, shape, cuts, least, top_value):
    def one(axis_at, parts):
        draws = jax.random.uniform(jax.random.fold_in(jax.random.fold_in(key, 6), axis_at), (parts,), jnp.float32, least / len(cuts), top_value / len(cuts))
        return jnp.repeat(jnp.exp(draws), shape[axis_at] // parts).reshape((-1,) + (1,) * (len(shape) - axis_at - 1))

    gain = one(*cuts[0])
    for cut in cuts[1:]:
        gain = gain * one(*cut)
    return gain


def noise(rng, extent, scale, bound, shards=(), dtype=jnp.bfloat16):
    array = jax.random.normal(rng, extent, jnp.float32) * scale
    if len(shards) > 0:
        array = level_of(rng, extent, shards, -0.22, 0.18) * array
    return jnp.clip(array, min=-bound, max=bound).astype(dtype)


def setup_inputs(seed: int = 0) -> dict:
    splits = jax.random.split(jax.random.key(seed), 10)
    return {
        "tracer": noise(splits[0], (2, TRC, LEV, NX, NY), 1.0, 6.0, ((0, 2), (3, 16)), jnp.float32),
        "velocity": jnp.clip(jax.random.uniform(splits[1], (2, 2, LEV, NX, NY), jnp.float32, -0.3, 0.3) * level_of(splits[1], (2, 2, LEV, NX, NY), ((0, 2), (3, 16)), -0.4, 0.0), -0.3, 0.3),
        "coupling": jnp.clip(jnp.exp(math.log(0.5) - 2.3025851 * jax.random.uniform(splits[2], (2, TRC, NX, NY), jnp.float32) ** level_of(splits[2], (2, TRC, NX, NY), ((0, 2), (2, 16)), -0.2, 0.2)), 0.05, 0.5),
        "sea_mask": with_ends((jax.random.randint(splits[3], (2, NX, NY), 0, 4) < 3).astype(jnp.int32), jax.random.fold_in(splits[3], 1), 0, 1),
        "send_rows": with_ends(jax.random.randint(splits[4], (2, N_TILE, NB, CAP), 0, CX), jax.random.fold_in(splits[4], 1), 0, CX - 1).astype(jnp.int32),
        "send_cols": with_ends(jax.random.randint(splits[5], (2, N_TILE, NB, CAP), 0, NY), jax.random.fold_in(splits[5], 1), 0, NY - 1).astype(jnp.int32),
        "intersection_near": with_ends(jax.random.randint(splits[6], (2, K, NX, NY), 0, NB), jax.random.fold_in(splits[6], 1), 0, NB - 1).astype(jnp.int32),
        "intersection_slot": with_ends(jax.random.randint(splits[7], (2, K, NX, NY), 0, CAP), jax.random.fold_in(splits[7], 1), 0, CAP - 1).astype(jnp.int32),
        "intersection_weight": draw_intersection_weight(jax.random.fold_in(splits[9], 71), 0),
    }


diffusion = 0.12


def substep(field, speed):
    east = jnp.roll(field, -1, axis=2)
    west = jnp.roll(field, 1, axis=2)
    north = jnp.roll(field, -1, axis=3)
    south = jnp.roll(field, 1, axis=3)
    return field - 0.5 * speed[0] * (east - west) - 0.5 * speed[1] * (north - south) + diffusion * (east + west + north + south - 4.0 * field)


def reference(tracer, velocity, coupling, sea_mask, send_rows, send_cols, intersection_near, intersection_slot, intersection_weight):
    results = []
    for comp in range(2):
        other = 1 - comp
        surface = tracer[other, :, 0].reshape(TRC, NX * NY)
        xpos = lax.broadcasted_iota(jnp.int32, (NX, NY), 0)
        dest_tile = xpos // CX
        remapped = jnp.zeros((TRC, NX, NY), jnp.float32)
        for k in range(K):
            near = intersection_near[comp, k]
            source = ((dest_tile + near - 1 + N_TILE) % N_TILE).astype(jnp.int32)
            within = intersection_slot[comp, k]
            row_local = send_rows[other][source, near, within]
            col_local = send_cols[other][source, near, within]
            cell = ((source * CX + row_local) * NY + col_local).astype(jnp.int32)
            picked = jnp.take(surface, cell.reshape(-1), axis=1).reshape(TRC, NX, NY)
            remapped = remapped + intersection_weight[comp, k] * picked
        level0 = tracer[comp, :, 0]
        masked = sea_mask[comp].astype(jnp.float32)
        new0 = level0 + coupling[comp] * masked * (remapped - level0)
        field = tracer[comp].at[:, 0].set(new0)
        speed = velocity[comp]
        for step in range(2):
            field = substep(field, speed)
        results.append(field)
    return jnp.stack(results)
```

```python
import functools

import jax
import jax.numpy as jnp
from jax import lax
from jax.experimental import pallas as pl
from jax.experimental.pallas import tpu as pltpu
from jax.sharding import PartitionSpec as P

diffusion = 0.12
LANES = 128
MESH = pl.DeviceIdType.MESH


def lane_pick(table, lanes):
    return jnp.take_along_axis(table, lanes, axis=1, mode="promise_in_bounds")


def pick_blocks(blocks, his, los, tracers):
    halves = tracers // 8
    picked = [[jnp.zeros((8, LANES), jnp.float32)] * halves for _ in his]
    for ident, load in blocks:
        parts = [load(half) for half in range(halves)]
        for n, (hi, lo) in enumerate(zip(his, los)):
            hit = hi == ident
            for half in range(halves):
                picked[n][half] = jnp.where(
                    hit, lane_pick(parts[half], lo), picked[n][half]
                )
    return picked


def exchange_kernel(
    dims,
    tracer_ref,
    vel_ref,
    coup_ref,
    mask_ref,
    rows_ref,
    cols_ref,
    near_ref,
    slot_ref,
    weight_ref,
    out_ref,
    lev_ref,
    vel_buf,
    packed,
    received,
    total,
    first,
    pack_send,
    pack_recv,
    halo_send,
    halo_recv,
    edge_send,
    edge_recv,
    vel_send,
    vel_recv,
):
    tiles, tracers, levels, rows, chunks, nears, blocks, inters = dims
    groups = rows * chunks
    halves = tracers // 8
    me_c = lax.axis_index("comp")
    me_t = lax.axis_index("tile")
    other = 1 - me_c

    def tile_at(step):
        return lax.rem(me_t + step + tiles, tiles)

    up, down = tile_at(1), tile_at(-1)
    steps = sorted({1 - j for j in range(nears)} | {j - 1 for j in range(nears)})
    barrier = pltpu.get_barrier_semaphore()
    for step in steps:
        pl.semaphore_signal(
            barrier, inc=1, device_id=(other, tile_at(step)), device_id_type=MESH
        )
    for side in (up, down):
        pl.semaphore_signal(barrier, inc=1, device_id=(me_c, side), device_id_type=MESH)

    def load_level(level):
        def one(g, _):
            c, r = g // rows, g % rows
            lev_ref[level, 2 + r, c] = tracer_ref[
                pl.ds(level * groups + g, tracers, stride=levels * groups), :
            ]
            return 0

        lax.fori_loop(0, groups, one, 0)

    load_level(0)

    def wide(ref, row):
        return jnp.broadcast_to(ref[pl.ds(row, 1), :], (8, LANES))

    def pack(j):
        batch = 4

        def one(b, _):
            his, los = [], []
            for n in range(batch):
                at = (b * batch + n) * nears + j
                row, col = wide(rows_ref, at), wide(cols_ref, at)
                his.append(row * chunks + (col >> 7))
                los.append(col & 127)
            table = [
                (
                    r * chunks + c,
                    lambda half, r=r, c=c: lev_ref[0, 2 + r, c, pl.ds(half * 8, 8), :],
                )
                for r in range(rows)
                for c in range(chunks)
            ]
            picked = pick_blocks(table, his, los, tracers)
            for n in range(batch):
                for half in range(halves):
                    packed[j, b * batch + n, pl.ds(half * 8, 8), :] = picked[n][half]
            return 0

        lax.fori_loop(0, blocks // batch, one, 0)

    order = [1] + [j for j in range(nears) if j != 1]
    pack_copies = {}
    for at, j in enumerate(order[1:] + order[:1]):
        pack(j)
        if at == 0:
            pl.semaphore_wait(barrier, len(steps) + 2)
        pack_copies[j] = pltpu.make_async_remote_copy(
            src_ref=packed.at[j],
            dst_ref=received.at[j],
            send_sem=pack_send.at[j],
            recv_sem=pack_recv.at[j],
            device_id=(other, tile_at(1 - j)),
            device_id_type=MESH,
        )
        pack_copies[j].start()

    for level in range(1, levels):
        load_level(level)

    def load_velocity(i, _):
        for c in range(chunks):
            for r in range(rows):
                vel_buf[1 + r, i, c] = vel_ref[pl.ds(i * groups + c * rows + r, 1), :]
        return 0

    lax.fori_loop(0, 2 * levels, load_velocity, 0)

    def to_side(src, dst, send, recv, side):
        copy = pltpu.make_async_remote_copy(
            src_ref=src,
            dst_ref=dst,
            send_sem=send,
            recv_sem=recv,
            device_id=(me_c, side),
            device_id_type=MESH,
        )
        copy.start()
        return copy

    inner = pl.ds(1, levels - 1)
    low, high = pl.ds(0, 2), pl.ds(rows + 2, 2)
    own_low, own_high = pl.ds(2, 2), pl.ds(rows, 2)
    side_copies = [
        to_side(
            lev_ref.at[inner, own_low],
            lev_ref.at[inner, high],
            halo_send.at[0],
            halo_recv.at[0],
            down,
        ),
        to_side(
            lev_ref.at[inner, own_high],
            lev_ref.at[inner, low],
            halo_send.at[1],
            halo_recv.at[1],
            up,
        ),
        to_side(
            vel_buf.at[1], vel_buf.at[rows + 1], vel_send.at[0], vel_recv.at[0], down
        ),
        to_side(vel_buf.at[rows], vel_buf.at[0], vel_send.at[1], vel_recv.at[1], up),
    ]

    def remap(r, c, nears_now):
        g = c * rows + r
        his, los = [], []
        for k in range(inters):
            near, slot = wide(near_ref, k * groups + g), wide(slot_ref, k * groups + g)
            his.append(near * blocks + (slot >> 7))
            los.append(slot & 127)
        table = [
            (
                j * blocks + b,
                lambda half, j=j, b=b: received[j, b, pl.ds(half * 8, 8), :],
            )
            for j in nears_now
            for b in range(blocks)
        ]
        picked = pick_blocks(table, his, los, tracers)
        sums = [jnp.zeros((8, LANES), jnp.float32)] * halves
        for k in range(inters):
            weight = wide(weight_ref, k * groups + g)
            sums = [sums[half] + weight * picked[k][half] for half in range(halves)]
        return sums

    def couple(r, c, sums):
        g = c * rows + r
        mask = wide(mask_ref, g).astype(jnp.float32)
        coup = coup_ref[pl.ds(g, tracers, stride=groups), :]
        for half in range(halves):
            at = pl.ds(half * 8, 8)
            old = lev_ref[0, 2 + r, c, at, :]
            part = coup[half * 8 : half * 8 + 8]
            lev_ref[0, 2 + r, c, at, :] = old + part * mask * (sums[half] - old)

    for at, j in enumerate(order):
        pack_copies[j].wait_recv()
        last = at == nears - 1

        def one(g, _, j=j, at=at, last=last):
            r, c = g // chunks, g % chunks
            sums = remap(r, c, [j])
            for half in range(halves):
                rows8 = pl.ds(half * 8, 8)
                if at > 0:
                    sums[half] = sums[half] + total[g, rows8, :]
                if not last:
                    total[g, rows8, :] = sums[half]
            if last:
                couple(r, c, sums)
            return 0

        lax.fori_loop(0, 2 * chunks, one, 0)
    edge_copies = [
        to_side(
            lev_ref.at[0, own_low],
            lev_ref.at[0, high],
            edge_send.at[0],
            edge_recv.at[0],
            down,
        )
    ]
    for r in range(2, rows):

        def one(c, _, r=r):
            couple(r, c, remap(r, c, order))
            return 0

        lax.fori_loop(0, chunks, one, 0)
        if r >= rows - 2:
            n = r - (rows - 2)
            edge_copies.append(
                to_side(
                    lev_ref.at[0, 2 + r],
                    lev_ref.at[0, n],
                    edge_send.at[1 + n],
                    edge_recv.at[1 + n],
                    up,
                )
            )

    lane = lax.broadcasted_iota(jnp.int32, (chunks * tracers, LANES), 1)

    def stepped(field, east, west, level, vrow):
        flat = field.reshape(chunks * tracers, LANES)
        ahead = pltpu.roll(flat, LANES - 1, 1)
        behind = pltpu.roll(flat, 1, 1)
        north = jnp.where(
            lane == LANES - 1,
            jnp.concatenate([ahead[tracers:], ahead[:tracers]], axis=0),
            ahead,
        ).reshape(chunks, tracers, LANES)
        south = jnp.where(
            lane == 0,
            jnp.concatenate([behind[-tracers:], behind[:-tracers]], axis=0),
            behind,
        ).reshape(chunks, tracers, LANES)
        u = vel_buf[vrow, level]
        v = vel_buf[vrow, levels + level]
        return (
            field
            - 0.5 * u * (east - west)
            - 0.5 * v * (north - south)
            + diffusion * (east + west + north + south - 4.0 * field)
        )

    def transport(level):
        def step_one(i, _):
            first[i] = stepped(
                lev_ref[level, i + 1],
                lev_ref[level, i + 2],
                lev_ref[level, i],
                level,
                i,
            )
            return 0

        lax.fori_loop(0, rows + 2, step_one, 0)

        def step_two(r, _):
            value = stepped(first[r + 1], first[r + 2], first[r], level, r + 1)
            for c in range(chunks):
                out_ref[
                    pl.ds(
                        level * groups + c * rows + r, tracers, stride=levels * groups
                    ),
                    :,
                ] = value[c]
            return 0

        lax.fori_loop(0, rows, step_two, 0)

    for copy in side_copies:
        copy.wait()

    def inner_level(level, _):
        transport(level)
        return 0

    lax.fori_loop(1, levels, inner_level, 0)
    for copy in edge_copies:
        copy.wait()
    transport(0)
    for j in order:
        pack_copies[j].wait_send()


def split_rows(x):
    *lead, rows, width = x.shape
    chunks = width // LANES
    x = jnp.swapaxes(x.reshape(*lead, rows, chunks, LANES), -3, -2)
    return x.reshape(-1, LANES)


def per_device(
    tiles,
    tracer,
    velocity,
    coupling,
    sea_mask,
    send_rows,
    send_cols,
    intersection_near,
    intersection_slot,
    intersection_weight,
):
    _, tracers, levels, rows, width = tracer.shape
    nears, capacity = send_rows.shape[2:]
    inters = intersection_slot.shape[1]
    chunks, blocks = width // LANES, capacity // LANES
    dims = (tiles, tracers, levels, rows, chunks, nears, blocks, inters)
    dma = pltpu.SemaphoreType.DMA
    vmem = pl.BlockSpec(memory_space=pltpu.VMEM)
    f32 = jnp.float32
    out = pl.pallas_call(
        functools.partial(exchange_kernel, dims),
        out_shape=jax.ShapeDtypeStruct((tracers * levels * rows * chunks, LANES), f32),
        in_specs=[vmem] * 9,
        out_specs=vmem,
        scratch_shapes=[
            pltpu.VMEM((levels, rows + 4, chunks, tracers, LANES), f32),
            pltpu.VMEM((rows + 2, 2 * levels, chunks, 1, LANES), f32),
            pltpu.VMEM((nears, blocks, tracers, LANES), f32),
            pltpu.VMEM((nears, blocks, tracers, LANES), f32),
            pltpu.VMEM((2 * chunks, tracers, LANES), f32),
            pltpu.VMEM((rows + 2, chunks, tracers, LANES), f32),
            dma((nears,)),
            dma((nears,)),
            dma((2,)),
            dma((2,)),
            dma((3,)),
            dma((3,)),
            dma((2,)),
            dma((2,)),
        ],
        compiler_params=pltpu.CompilerParams(collective_id=0, has_side_effects=True),
    )(
        split_rows(tracer),
        split_rows(velocity),
        split_rows(coupling),
        split_rows(sea_mask),
        split_rows(send_rows),
        split_rows(send_cols),
        split_rows(intersection_near),
        split_rows(intersection_slot),
        split_rows(intersection_weight),
    )
    out = out.reshape(1, tracers, levels, chunks, rows, LANES)
    return jnp.swapaxes(out, 3, 4).reshape(tracer.shape)


def solution(mesh):
    in_specs = (
        P("comp", None, None, "tile", None),
        P("comp", None, None, "tile", None),
        P("comp", None, "tile", None),
        P("comp", "tile", None),
        P("comp", "tile", None, None),
        P("comp", "tile", None, None),
        P("comp", None, "tile", None),
        P("comp", None, "tile", None),
        P("comp", None, "tile", None),
    )
    out_specs = P("comp", None, None, "tile", None)
    return jax.shard_map(
        functools.partial(per_device, mesh.shape["tile"]),
        mesh=mesh,
        in_specs=in_specs,
        out_specs=out_specs,
        check_vma=False,
    )
```

```python
import functools

import jax
import jax.numpy as jnp
from jax import lax
from jax.experimental import pallas as pl
from jax.experimental.pallas import tpu as pltpu
from jax.sharding import PartitionSpec as P

diffusion = 0.12
LANES = 128
MESH = pl.DeviceIdType.MESH


def lane_pick(table, lanes):
    return jnp.take_along_axis(table, lanes, axis=1, mode="promise_in_bounds")


def pick_blocks(blocks, his, los, tracers):
    halves = tracers // 8
    picked = []
    for hi, lo in zip(his, los):
        chains = [[jnp.zeros((8, LANES), jnp.float32)] * 2 for _ in range(halves)]
        for n, (ident, load) in enumerate(blocks):
            hit = hi == ident
            for half in range(halves):
                chain = chains[half]
                chain[n % 2] = jnp.where(hit, lane_pick(load(half), lo), chain[n % 2])
        picked.append([one + two for one, two in chains])
    return picked


def exchange_kernel(
    dims,
    tracer_ref,
    vel_ref,
    coup_ref,
    mask_ref,
    rows_ref,
    cols_ref,
    near_ref,
    slot_ref,
    weight_ref,
    out_ref,
    lev_ref,
    vel_buf,
    packed,
    received,
    total,
    first,
    pack_send,
    pack_recv,
    halo_send,
    halo_recv,
    edge_send,
    edge_recv,
    vel_send,
    vel_recv,
):
    tiles, tracers, levels, rows, chunks, nears, blocks, inters = dims
    groups = rows * chunks
    halves = tracers // 8
    me_c = lax.axis_index("comp")
    me_t = lax.axis_index("tile")
    other = 1 - me_c

    def tile_at(step):
        return lax.rem(me_t + step + tiles, tiles)

    up, down = tile_at(1), tile_at(-1)
    steps = sorted({1 - j for j in range(nears)} | {j - 1 for j in range(nears)})
    barrier = pltpu.get_barrier_semaphore()
    for step in steps:
        pl.semaphore_signal(
            barrier, inc=1, device_id=(other, tile_at(step)), device_id_type=MESH
        )
    for side in (up, down):
        pl.semaphore_signal(barrier, inc=1, device_id=(me_c, side), device_id_type=MESH)

    def load_level(level):
        def one(g, _):
            c, r = g // rows, g % rows
            lev_ref[level, 2 + r, c] = tracer_ref[
                pl.ds(level * groups + g, tracers, stride=levels * groups), :
            ]
            return 0

        lax.fori_loop(0, groups, one, 0)

    load_level(0)

    def wide(ref, row):
        return jnp.broadcast_to(ref[pl.ds(row, 1), :], (8, LANES))

    def pack(j):
        batch = 4

        def one(b, _):
            his, los = [], []
            for n in range(batch):
                at = (b * batch + n) * nears + j
                row, col = wide(rows_ref, at), wide(cols_ref, at)
                his.append(row * chunks + (col >> 7))
                los.append(col & 127)
            table = [
                (
                    r * chunks + c,
                    lambda half, r=r, c=c: lev_ref[0, 2 + r, c, pl.ds(half * 8, 8), :],
                )
                for r in range(rows)
                for c in range(chunks)
            ]
            picked = pick_blocks(table, his, los, tracers)
            for n in range(batch):
                for half in range(halves):
                    packed[j, b * batch + n, pl.ds(half * 8, 8), :] = picked[n][half]
            return 0

        lax.fori_loop(0, blocks // batch, one, 0)

    order = [1] + [j for j in range(nears) if j != 1]
    pack_copies = {}
    for at, j in enumerate(order[1:] + order[:1]):
        pack(j)
        if at == 0:
            pl.semaphore_wait(barrier, len(steps) + 2)
        pack_copies[j] = pltpu.make_async_remote_copy(
            src_ref=packed.at[j],
            dst_ref=received.at[j],
            send_sem=pack_send.at[j],
            recv_sem=pack_recv.at[j],
            device_id=(other, tile_at(1 - j)),
            device_id_type=MESH,
        )
        pack_copies[j].start()

    for level in range(1, levels):
        load_level(level)

    def load_velocity(i, _):
        for c in range(chunks):
            for r in range(rows):
                vel_buf[1 + r, i, c] = vel_ref[pl.ds(i * groups + c * rows + r, 1), :]
        return 0

    lax.fori_loop(0, 2 * levels, load_velocity, 0)

    def to_side(src, dst, send, recv, side):
        copy = pltpu.make_async_remote_copy(
            src_ref=src,
            dst_ref=dst,
            send_sem=send,
            recv_sem=recv,
            device_id=(me_c, side),
            device_id_type=MESH,
        )
        copy.start()
        return copy

    inner = pl.ds(1, levels - 1)
    low, high = pl.ds(0, 2), pl.ds(rows + 2, 2)
    own_low, own_high = pl.ds(2, 2), pl.ds(rows, 2)
    side_copies = [
        to_side(
            lev_ref.at[inner, own_low],
            lev_ref.at[inner, high],
            halo_send.at[0],
            halo_recv.at[0],
            down,
        ),
        to_side(
            lev_ref.at[inner, own_high],
            lev_ref.at[inner, low],
            halo_send.at[1],
            halo_recv.at[1],
            up,
        ),
        to_side(
            vel_buf.at[1], vel_buf.at[rows + 1], vel_send.at[0], vel_recv.at[0], down
        ),
        to_side(vel_buf.at[rows], vel_buf.at[0], vel_send.at[1], vel_recv.at[1], up),
    ]

    def remap(r, c, nears_now):
        g = c * rows + r
        his, los = [], []
        for k in range(inters):
            near, slot = wide(near_ref, k * groups + g), wide(slot_ref, k * groups + g)
            his.append(near * blocks + (slot >> 7))
            los.append(slot & 127)
        table = [
            (
                j * blocks + b,
                lambda half, j=j, b=b: received[j, b, pl.ds(half * 8, 8), :],
            )
            for j in nears_now
            for b in range(blocks)
        ]
        picked = pick_blocks(table, his, los, tracers)
        sums = [jnp.zeros((8, LANES), jnp.float32)] * halves
        for k in range(inters):
            weight = wide(weight_ref, k * groups + g)
            sums = [sums[half] + weight * picked[k][half] for half in range(halves)]
        return sums

    def couple(r, c, sums):
        g = c * rows + r
        mask = wide(mask_ref, g).astype(jnp.float32)
        coup = coup_ref[pl.ds(g, tracers, stride=groups), :]
        for half in range(halves):
            at = pl.ds(half * 8, 8)
            old = lev_ref[0, 2 + r, c, at, :]
            part = coup[half * 8 : half * 8 + 8]
            lev_ref[0, 2 + r, c, at, :] = old + part * mask * (sums[half] - old)

    for at, j in enumerate(order):
        pack_copies[j].wait_recv()
        last = at == nears - 1

        def one(g, _, j=j, at=at, last=last):
            r, c = g // chunks, g % chunks
            sums = remap(r, c, [j])
            for half in range(halves):
                rows8 = pl.ds(half * 8, 8)
                if at > 0:
                    sums[half] = sums[half] + total[g, rows8, :]
                if not last:
                    total[g, rows8, :] = sums[half]
            if last:
                couple(r, c, sums)
            return 0

        lax.fori_loop(0, 2 * chunks, one, 0)
    edge_copies = [
        to_side(
            lev_ref.at[0, own_low],
            lev_ref.at[0, high],
            edge_send.at[0],
            edge_recv.at[0],
            down,
        )
    ]
    for r in range(2, rows):

        def one(c, _, r=r):
            couple(r, c, remap(r, c, order))
            return 0

        lax.fori_loop(0, chunks, one, 0)
        if r >= rows - 2:
            n = r - (rows - 2)
            edge_copies.append(
                to_side(
                    lev_ref.at[0, 2 + r],
                    lev_ref.at[0, n],
                    edge_send.at[1 + n],
                    edge_recv.at[1 + n],
                    up,
                )
            )

    lane = lax.broadcasted_iota(jnp.int32, (chunks * tracers, LANES), 1)

    def stepped(field, east, west, level, vrow):
        flat = field.reshape(chunks * tracers, LANES)
        ahead = pltpu.roll(flat, LANES - 1, 1)
        behind = pltpu.roll(flat, 1, 1)
        north = jnp.where(
            lane == LANES - 1,
            jnp.concatenate([ahead[tracers:], ahead[:tracers]], axis=0),
            ahead,
        ).reshape(chunks, tracers, LANES)
        south = jnp.where(
            lane == 0,
            jnp.concatenate([behind[-tracers:], behind[:-tracers]], axis=0),
            behind,
        ).reshape(chunks, tracers, LANES)
        u = vel_buf[vrow, level]
        v = vel_buf[vrow, levels + level]
        return (
            field
            - 0.5 * u * (east - west)
            - 0.5 * v * (north - south)
            + diffusion * (east + west + north + south - 4.0 * field)
        )

    def transport(level):
        def step_one(i, _):
            first[i] = stepped(
                lev_ref[level, i + 1],
                lev_ref[level, i + 2],
                lev_ref[level, i],
                level,
                i,
            )
            return 0

        lax.fori_loop(0, rows + 2, step_one, 0)

        def step_two(r, _):
            value = stepped(first[r + 1], first[r + 2], first[r], level, r + 1)
            for c in range(chunks):
                out_ref[
                    pl.ds(
                        level * groups + c * rows + r, tracers, stride=levels * groups
                    ),
                    :,
                ] = value[c]
            return 0

        lax.fori_loop(0, rows, step_two, 0)

    for copy in side_copies:
        copy.wait()

    def inner_level(level, _):
        transport(level)
        return 0

    lax.fori_loop(1, levels, inner_level, 0)
    for copy in edge_copies:
        copy.wait()
    transport(0)
    for j in order:
        pack_copies[j].wait_send()


def split_rows(x):
    *lead, rows, width = x.shape
    chunks = width // LANES
    x = jnp.swapaxes(x.reshape(*lead, rows, chunks, LANES), -3, -2)
    return x.reshape(-1, LANES)


def per_device(
    tiles,
    tracer,
    velocity,
    coupling,
    sea_mask,
    send_rows,
    send_cols,
    intersection_near,
    intersection_slot,
    intersection_weight,
):
    _, tracers, levels, rows, width = tracer.shape
    nears, capacity = send_rows.shape[2:]
    inters = intersection_slot.shape[1]
    chunks, blocks = width // LANES, capacity // LANES
    dims = (tiles, tracers, levels, rows, chunks, nears, blocks, inters)
    dma = pltpu.SemaphoreType.DMA
    vmem = pl.BlockSpec(memory_space=pltpu.VMEM)
    f32 = jnp.float32
    out = pl.pallas_call(
        functools.partial(exchange_kernel, dims),
        out_shape=jax.ShapeDtypeStruct((tracers * levels * rows * chunks, LANES), f32),
        in_specs=[vmem] * 9,
        out_specs=vmem,
        scratch_shapes=[
            pltpu.VMEM((levels, rows + 4, chunks, tracers, LANES), f32),
            pltpu.VMEM((rows + 2, 2 * levels, chunks, 1, LANES), f32),
            pltpu.VMEM((nears, blocks, tracers, LANES), f32),
            pltpu.VMEM((nears, blocks, tracers, LANES), f32),
            pltpu.VMEM((2 * chunks, tracers, LANES), f32),
            pltpu.VMEM((rows + 2, chunks, tracers, LANES), f32),
            dma((nears,)),
            dma((nears,)),
            dma((2,)),
            dma((2,)),
            dma((3,)),
            dma((3,)),
            dma((2,)),
            dma((2,)),
        ],
        compiler_params=pltpu.CompilerParams(collective_id=0, has_side_effects=True),
    )(
        split_rows(tracer),
        split_rows(velocity),
        split_rows(coupling),
        split_rows(sea_mask),
        split_rows(send_rows),
        split_rows(send_cols),
        split_rows(intersection_near),
        split_rows(intersection_slot),
        split_rows(intersection_weight),
    )
    out = out.reshape(1, tracers, levels, chunks, rows, LANES)
    return jnp.swapaxes(out, 3, 4).reshape(tracer.shape)


def solution(mesh):
    in_specs = (
        P("comp", None, None, "tile", None),
        P("comp", None, None, "tile", None),
        P("comp", None, "tile", None),
        P("comp", "tile", None),
        P("comp", "tile", None, None),
        P("comp", "tile", None, None),
        P("comp", None, "tile", None),
        P("comp", None, "tile", None),
        P("comp", None, "tile", None),
    )
    out_specs = P("comp", None, None, "tile", None)
    return jax.shard_map(
        functools.partial(per_device, mesh.shape["tile"]),
        mesh=mesh,
        in_specs=in_specs,
        out_specs=out_specs,
        check_vma=False,
    )
```

```python
import functools

import jax
import jax.numpy as jnp
from jax import lax
from jax.experimental import pallas as pl
from jax.experimental.pallas import tpu as pltpu
from jax.sharding import PartitionSpec as P

diffusion = 0.12
LANES = 128
MESH = pl.DeviceIdType.MESH
PAIR = 2
ON_LANES = 2


def lane_pick(table, lanes):
    return jnp.take_along_axis(table, lanes, axis=1, mode="promise_in_bounds")


def pick_blocks(blocks, his, los, tracers):
    halves = tracers // 8
    picked = []
    for hi, lo in zip(his, los):
        chains = [[jnp.zeros((8, LANES), jnp.float32)] * 2 for _ in range(halves)]
        for n, (ident, load) in enumerate(blocks):
            hit = hi == ident
            for half in range(halves):
                chain = chains[half]
                chain[n % 2] = jnp.where(hit, lane_pick(load(half), lo), chain[n % 2])
        picked.append([one + two for one, two in chains])
    return picked


def split_pieces(value, pieces, block, tracers):
    top = value.astype(jnp.bfloat16)
    rest = (value - top.astype(jnp.float32)).astype(jnp.bfloat16)
    rows_at = pl.ds(block * tracers, tracers)
    pieces[rows_at, pl.ds(0, LANES)] = top
    pieces[rows_at, pl.ds(LANES, LANES)] = rest


def dot_blocks(left, his, los, tracers):
    halves = tracers // 8
    count = left.shape[0] // tracers
    lane_id = lax.broadcasted_iota(jnp.int32, (LANES, LANES), 0)
    picked = []
    for k in range(0, len(his), PAIR):
        hots = []
        for lo in los[k : k + PAIR]:
            hot = lane_id == jnp.broadcast_to(lo, (LANES, LANES))
            hot = hot.astype(jnp.float32).astype(jnp.bfloat16)
            hots.append(jnp.concatenate([hot, hot], axis=0))
        found = jnp.dot(
            left, jnp.concatenate(hots, axis=1), preferred_element_type=jnp.float32
        )
        for n, hi in enumerate(his[k : k + PAIR]):
            hi = jnp.broadcast_to(hi, (8, LANES))
            part = [jnp.zeros((8, LANES), jnp.float32)] * halves
            for block in range(count):
                hit = hi == block
                for half in range(halves):
                    row = block * tracers + half * 8
                    cell = found[row : row + 8, n * LANES : (n + 1) * LANES]
                    part[half] = jnp.where(hit, cell, part[half])
            picked.append(part)
    return picked


def exchange_kernel(
    dims,
    tracer_ref,
    vel_ref,
    coup_ref,
    mask_ref,
    rows_ref,
    cols_ref,
    near_ref,
    slot_ref,
    weight_ref,
    out_ref,
    lev_ref,
    vel_buf,
    packed,
    received,
    first,
    pieces,
    surface_pieces,
    pack_send,
    pack_recv,
    halo_send,
    halo_recv,
    edge_send,
    edge_recv,
    vel_send,
    vel_recv,
):
    tiles, tracers, levels, rows, chunks, nears, blocks, inters = dims
    groups = rows * chunks
    halves = tracers // 8
    me_c = lax.axis_index("comp")
    me_t = lax.axis_index("tile")
    other = 1 - me_c

    def tile_at(step):
        return lax.rem(me_t + step + tiles, tiles)

    up, down = tile_at(1), tile_at(-1)
    steps = sorted({1 - j for j in range(nears)} | {j - 1 for j in range(nears)})
    barrier = pltpu.get_barrier_semaphore()
    for step in steps:
        pl.semaphore_signal(
            barrier, inc=1, device_id=(other, tile_at(step)), device_id_type=MESH
        )
    for side in (up, down):
        pl.semaphore_signal(barrier, inc=1, device_id=(me_c, side), device_id_type=MESH)

    def load_level(level):
        def one(g, _):
            c, r = g // rows, g % rows
            lev_ref[level, 2 + r, c] = tracer_ref[
                pl.ds(level * groups + g, tracers, stride=levels * groups), :
            ]
            return 0

        lax.fori_loop(0, groups, one, 0)

    load_level(0)

    def wide(ref, row):
        return jnp.broadcast_to(ref[pl.ds(row, 1), :], (8, LANES))

    for r in range(rows):
        for c in range(chunks):
            split_pieces(lev_ref[0, 2 + r, c], surface_pieces, r * chunks + c, tracers)

    def pack(j):
        batch = 4

        def one(b, _):
            his, los = [], []
            for n in range(batch):
                at = (b * batch + n) * nears + j
                row, col = rows_ref[pl.ds(at, 1), :], cols_ref[pl.ds(at, 1), :]
                his.append(row * chunks + (col >> 7))
                los.append(col & 127)
            picked = dot_blocks(surface_pieces[...], his, los, tracers)
            for n in range(batch):
                for half in range(halves):
                    packed[j, b * batch + n, pl.ds(half * 8, 8), :] = picked[n][half]
            return 0

        lax.fori_loop(0, blocks // batch, one, 0)

    order = [1] + [j for j in range(nears) if j != 1]
    pack_copies = {}
    for at, j in enumerate(order[1:] + order[:1]):
        pack(j)
        if at == 0:
            pl.semaphore_wait(barrier, len(steps) + 2)
        pack_copies[j] = pltpu.make_async_remote_copy(
            src_ref=packed.at[j],
            dst_ref=received.at[j],
            send_sem=pack_send.at[j],
            recv_sem=pack_recv.at[j],
            device_id=(other, tile_at(1 - j)),
            device_id_type=MESH,
        )
        pack_copies[j].start()

    for level in range(1, levels):
        load_level(level)

    def load_velocity(i, _):
        for c in range(chunks):
            for r in range(rows):
                vel_buf[1 + r, i, c] = vel_ref[pl.ds(i * groups + c * rows + r, 1), :]
        return 0

    lax.fori_loop(0, 2 * levels, load_velocity, 0)

    def to_side(src, dst, send, recv, side):
        copy = pltpu.make_async_remote_copy(
            src_ref=src,
            dst_ref=dst,
            send_sem=send,
            recv_sem=recv,
            device_id=(me_c, side),
            device_id_type=MESH,
        )
        copy.start()
        return copy

    inner = pl.ds(1, levels - 1)
    low, high = pl.ds(0, 2), pl.ds(rows + 2, 2)
    own_low, own_high = pl.ds(2, 2), pl.ds(rows, 2)
    side_copies = [
        to_side(
            lev_ref.at[inner, own_low],
            lev_ref.at[inner, high],
            halo_send.at[0],
            halo_recv.at[0],
            down,
        ),
        to_side(
            lev_ref.at[inner, own_high],
            lev_ref.at[inner, low],
            halo_send.at[1],
            halo_recv.at[1],
            up,
        ),
        to_side(
            vel_buf.at[1], vel_buf.at[rows + 1], vel_send.at[0], vel_recv.at[0], down
        ),
        to_side(vel_buf.at[rows], vel_buf.at[0], vel_send.at[1], vel_recv.at[1], up),
    ]

    def remap(r, c):
        g = c * rows + r
        table = [
            (
                j * blocks + b,
                lambda half, j=j, b=b: received[j, b, pl.ds(half * 8, 8), :],
            )
            for j in range(nears)
            for b in range(blocks)
        ]
        his, los, weights = [], [], []
        for k in range(inters):
            at = k * groups + g
            his.append(near_ref[pl.ds(at, 1), :] * blocks + (slot_ref[pl.ds(at, 1), :] >> 7))
            los.append(slot_ref[pl.ds(at, 1), :] & 127)
            weights.append(wide(weight_ref, at))
        on_mxu = inters - ON_LANES
        picked = dot_blocks(pieces[...], his[:on_mxu], los[:on_mxu], tracers)
        if ON_LANES > 0:
            picked += pick_blocks(
                table,
                [jnp.broadcast_to(x, (8, LANES)) for x in his[on_mxu:]],
                [jnp.broadcast_to(x, (8, LANES)) for x in los[on_mxu:]],
                tracers,
            )
        sums = [jnp.zeros((8, LANES), jnp.float32)] * halves
        for weight, part in zip(weights, picked):
            sums = [sums[half] + weight * part[half] for half in range(halves)]
        return sums

    def couple(r, c, sums):
        g = c * rows + r
        mask = wide(mask_ref, g).astype(jnp.float32)
        coup = coup_ref[pl.ds(g, tracers, stride=groups), :]
        for half in range(halves):
            at = pl.ds(half * 8, 8)
            old = lev_ref[0, 2 + r, c, at, :]
            part = coup[half * 8 : half * 8 + 8]
            lev_ref[0, 2 + r, c, at, :] = old + part * mask * (sums[half] - old)

    for j in order[1:] + order[:1]:
        pack_copies[j].wait_recv()

    def split_slots(b, _):
        for j in range(nears):
            split_pieces(received[j, b], pieces, j * blocks + b, tracers)
        return 0

    lax.fori_loop(0, blocks, split_slots, 0)

    def low_rows(g, _):
        couple(g // chunks, g % chunks, remap(g // chunks, g % chunks))
        return 0

    lax.fori_loop(0, 2 * chunks, low_rows, 0)
    edge_copies = [
        to_side(
            lev_ref.at[0, own_low],
            lev_ref.at[0, high],
            edge_send.at[0],
            edge_recv.at[0],
            down,
        )
    ]
    for r in range(2, rows):

        def one(c, _, r=r):
            couple(r, c, remap(r, c))
            return 0

        lax.fori_loop(0, chunks, one, 0)
        if r >= rows - 2:
            n = r - (rows - 2)
            edge_copies.append(
                to_side(
                    lev_ref.at[0, 2 + r],
                    lev_ref.at[0, n],
                    edge_send.at[1 + n],
                    edge_recv.at[1 + n],
                    up,
                )
            )

    lane = lax.broadcasted_iota(jnp.int32, (chunks * tracers, LANES), 1)

    def stepped(field, east, west, level, vrow):
        flat = field.reshape(chunks * tracers, LANES)
        ahead = pltpu.roll(flat, LANES - 1, 1)
        behind = pltpu.roll(flat, 1, 1)
        north = jnp.where(
            lane == LANES - 1,
            jnp.concatenate([ahead[tracers:], ahead[:tracers]], axis=0),
            ahead,
        ).reshape(chunks, tracers, LANES)
        south = jnp.where(
            lane == 0,
            jnp.concatenate([behind[-tracers:], behind[:-tracers]], axis=0),
            behind,
        ).reshape(chunks, tracers, LANES)
        u = vel_buf[vrow, level]
        v = vel_buf[vrow, levels + level]
        return (
            field
            - 0.5 * u * (east - west)
            - 0.5 * v * (north - south)
            + diffusion * (east + west + north + south - 4.0 * field)
        )

    def transport(level):
        def step_one(i, _):
            first[i] = stepped(
                lev_ref[level, i + 1],
                lev_ref[level, i + 2],
                lev_ref[level, i],
                level,
                i,
            )
            return 0

        lax.fori_loop(0, rows + 2, step_one, 0, unroll=2)

        def step_two(r, _):
            value = stepped(first[r + 1], first[r + 2], first[r], level, r + 1)
            for c in range(chunks):
                out_ref[
                    pl.ds(
                        level * groups + c * rows + r, tracers, stride=levels * groups
                    ),
                    :,
                ] = value[c]
            return 0

        lax.fori_loop(0, rows, step_two, 0, unroll=2)

    for copy in side_copies:
        copy.wait()

    def inner_level(level, _):
        transport(level)
        return 0

    lax.fori_loop(1, levels, inner_level, 0)
    for copy in edge_copies:
        copy.wait()
    transport(0)
    for j in order:
        pack_copies[j].wait_send()


def split_rows(x):
    *lead, rows, width = x.shape
    chunks = width // LANES
    x = jnp.swapaxes(x.reshape(*lead, rows, chunks, LANES), -3, -2)
    return x.reshape(-1, LANES)


def per_device(
    tiles,
    tracer,
    velocity,
    coupling,
    sea_mask,
    send_rows,
    send_cols,
    intersection_near,
    intersection_slot,
    intersection_weight,
):
    _, tracers, levels, rows, width = tracer.shape
    nears, capacity = send_rows.shape[2:]
    inters = intersection_slot.shape[1]
    chunks, blocks = width // LANES, capacity // LANES
    dims = (tiles, tracers, levels, rows, chunks, nears, blocks, inters)
    dma = pltpu.SemaphoreType.DMA
    vmem = pl.BlockSpec(memory_space=pltpu.VMEM)
    f32 = jnp.float32
    out = pl.pallas_call(
        functools.partial(exchange_kernel, dims),
        out_shape=jax.ShapeDtypeStruct((tracers * levels * rows * chunks, LANES), f32),
        in_specs=[vmem] * 9,
        out_specs=vmem,
        scratch_shapes=[
            pltpu.VMEM((levels, rows + 4, chunks, tracers, LANES), f32),
            pltpu.VMEM((rows + 2, 2 * levels, chunks, 1, LANES), f32),
            pltpu.VMEM((nears, blocks, tracers, LANES), f32),
            pltpu.VMEM((nears, blocks, tracers, LANES), f32),
            pltpu.VMEM((rows + 2, chunks, tracers, LANES), f32),
            pltpu.VMEM((nears * blocks * tracers, 2 * LANES), jnp.bfloat16),
            pltpu.VMEM((rows * chunks * tracers, 2 * LANES), jnp.bfloat16),
            dma((nears,)),
            dma((nears,)),
            dma((2,)),
            dma((2,)),
            dma((3,)),
            dma((3,)),
            dma((2,)),
            dma((2,)),
        ],
        compiler_params=pltpu.CompilerParams(collective_id=0, has_side_effects=True),
    )(
        split_rows(tracer),
        split_rows(velocity),
        split_rows(coupling),
        split_rows(sea_mask),
        split_rows(send_rows),
        split_rows(send_cols),
        split_rows(intersection_near),
        split_rows(intersection_slot),
        split_rows(intersection_weight),
    )
    out = out.reshape(1, tracers, levels, chunks, rows, LANES)
    return jnp.swapaxes(out, 3, 4).reshape(tracer.shape)


def solution(mesh):
    in_specs = (
        P("comp", None, None, "tile", None),
        P("comp", None, None, "tile", None),
        P("comp", None, "tile", None),
        P("comp", "tile", None),
        P("comp", "tile", None, None),
        P("comp", "tile", None, None),
        P("comp", None, "tile", None),
        P("comp", None, "tile", None),
        P("comp", None, "tile", None),
    )
    out_specs = P("comp", None, None, "tile", None)
    return jax.shard_map(
        functools.partial(per_device, mesh.shape["tile"]),
        mesh=mesh,
        in_specs=in_specs,
        out_specs=out_specs,
        check_vma=False,
    )
```

```python
import functools

import jax
import jax.numpy as jnp
from jax import lax
from jax.experimental import pallas as pl
from jax.experimental.pallas import tpu as pltpu
from jax.sharding import PartitionSpec as P

diffusion = 0.12
LANES = 128
MESH = pl.DeviceIdType.MESH
PAIR = 2
ON_LANES = 2


def lane_pick(table, lanes):
    return jnp.take_along_axis(table, lanes, axis=1, mode="promise_in_bounds")


def pick_blocks(blocks, his, los, tracers):
    halves = tracers // 8
    picked = []
    for hi, lo in zip(his, los):
        chains = [[jnp.zeros((8, LANES), jnp.float32)] * 2 for _ in range(halves)]
        for n, (ident, load) in enumerate(blocks):
            hit = hi == ident
            for half in range(halves):
                chain = chains[half]
                chain[n % 2] = jnp.where(hit, lane_pick(load(half), lo), chain[n % 2])
        picked.append([one + two for one, two in chains])
    return picked


def split_pieces(value, pieces, block, tracers):
    top = value.astype(jnp.bfloat16)
    rest = (value - top.astype(jnp.float32)).astype(jnp.bfloat16)
    rows_at = pl.ds(block * tracers, tracers)
    pieces[rows_at, pl.ds(0, LANES)] = top
    pieces[rows_at, pl.ds(LANES, LANES)] = rest


def dot_blocks(left, his, los, tracers):
    halves = tracers // 8
    count = left.shape[0] // tracers
    lane_id = lax.broadcasted_iota(jnp.int32, (LANES, LANES), 0)
    picked = []
    for k in range(0, len(his), PAIR):
        hots = []
        for lo in los[k : k + PAIR]:
            hot = lane_id == jnp.broadcast_to(lo, (LANES, LANES))
            hot = hot.astype(jnp.float32).astype(jnp.bfloat16)
            hots.append(jnp.concatenate([hot, hot], axis=0))
        found = jnp.dot(
            left, jnp.concatenate(hots, axis=1), preferred_element_type=jnp.float32
        )
        for n, hi in enumerate(his[k : k + PAIR]):
            hi = jnp.broadcast_to(hi, (8, LANES))
            part = [jnp.zeros((8, LANES), jnp.float32)] * halves
            for block in range(count):
                hit = hi == block
                for half in range(halves):
                    row = block * tracers + half * 8
                    cell = found[row : row + 8, n * LANES : (n + 1) * LANES]
                    part[half] = jnp.where(hit, cell, part[half])
            picked.append(part)
    return picked


def exchange_kernel(
    dims,
    tracer_ref,
    vel_ref,
    coup_ref,
    mask_ref,
    rows_ref,
    cols_ref,
    near_ref,
    slot_ref,
    weight_ref,
    out_ref,
    lev_ref,
    vel_buf,
    packed,
    received,
    first,
    pieces,
    surface_pieces,
    pack_send,
    pack_recv,
    halo_send,
    halo_recv,
    edge_send,
    edge_recv,
    vel_send,
    vel_recv,
):
    tiles, tracers, levels, rows, chunks, nears, blocks, inters = dims
    groups = rows * chunks
    halves = tracers // 8
    me_c = lax.axis_index("comp")
    me_t = lax.axis_index("tile")
    other = 1 - me_c

    def tile_at(step):
        return lax.rem(me_t + step + tiles, tiles)

    up, down = tile_at(1), tile_at(-1)
    steps = sorted({1 - j for j in range(nears)} | {j - 1 for j in range(nears)})
    barrier = pltpu.get_barrier_semaphore()
    for step in steps:
        pl.semaphore_signal(
            barrier, inc=1, device_id=(other, tile_at(step)), device_id_type=MESH
        )
    for side in (up, down):
        pl.semaphore_signal(barrier, inc=1, device_id=(me_c, side), device_id_type=MESH)

    def load_level(level):
        def one(g, _):
            c, r = g // rows, g % rows
            lev_ref[level, 2 + r, c] = tracer_ref[
                pl.ds(level * groups + g, tracers, stride=levels * groups), :
            ]
            return 0

        lax.fori_loop(0, groups, one, 0)

    load_level(0)

    def wide(ref, row):
        return jnp.broadcast_to(ref[pl.ds(row, 1), :], (8, LANES))

    for r in range(rows):
        for c in range(chunks):
            split_pieces(lev_ref[0, 2 + r, c], surface_pieces, r * chunks + c, tracers)

    def pack(j):
        batch = 8

        def one(b, _):
            his, los = [], []
            for n in range(batch):
                at = (b * batch + n) * nears + j
                row, col = rows_ref[pl.ds(at, 1), :], cols_ref[pl.ds(at, 1), :]
                his.append(row * chunks + (col >> 7))
                los.append(col & 127)
            on_mxu = batch - 2
            picked = dot_blocks(surface_pieces[...], his[:on_mxu], los[:on_mxu], tracers)
            table = [
                (
                    r * chunks + c,
                    lambda half, r=r, c=c: lev_ref[0, 2 + r, c, pl.ds(half * 8, 8), :],
                )
                for r in range(rows)
                for c in range(chunks)
            ]
            picked += pick_blocks(
                table,
                [jnp.broadcast_to(x, (8, LANES)) for x in his[on_mxu:]],
                [jnp.broadcast_to(x, (8, LANES)) for x in los[on_mxu:]],
                tracers,
            )
            for n in range(batch):
                for half in range(halves):
                    packed[j, b * batch + n, pl.ds(half * 8, 8), :] = picked[n][half]
            return 0

        lax.fori_loop(0, blocks // batch, one, 0)

    order = [1] + [j for j in range(nears) if j != 1]
    pack_copies = {}
    for at, j in enumerate(order[1:] + order[:1]):
        pack(j)
        if at == 0:
            pl.semaphore_wait(barrier, len(steps) + 2)
        pack_copies[j] = pltpu.make_async_remote_copy(
            src_ref=packed.at[j],
            dst_ref=received.at[j],
            send_sem=pack_send.at[j],
            recv_sem=pack_recv.at[j],
            device_id=(other, tile_at(1 - j)),
            device_id_type=MESH,
        )
        pack_copies[j].start()

    for level in range(1, levels):
        load_level(level)

    def load_velocity(i, _):
        for c in range(chunks):
            for r in range(rows):
                vel_buf[1 + r, i, c] = vel_ref[pl.ds(i * groups + c * rows + r, 1), :]
        return 0

    lax.fori_loop(0, 2 * levels, load_velocity, 0)

    def to_side(src, dst, send, recv, side):
        copy = pltpu.make_async_remote_copy(
            src_ref=src,
            dst_ref=dst,
            send_sem=send,
            recv_sem=recv,
            device_id=(me_c, side),
            device_id_type=MESH,
        )
        copy.start()
        return copy

    inner = pl.ds(1, levels - 1)
    low, high = pl.ds(0, 2), pl.ds(rows + 2, 2)
    own_low, own_high = pl.ds(2, 2), pl.ds(rows, 2)
    side_copies = [
        to_side(
            lev_ref.at[inner, own_low],
            lev_ref.at[inner, high],
            halo_send.at[0],
            halo_recv.at[0],
            down,
        ),
        to_side(
            lev_ref.at[inner, own_high],
            lev_ref.at[inner, low],
            halo_send.at[1],
            halo_recv.at[1],
            up,
        ),
        to_side(
            vel_buf.at[1], vel_buf.at[rows + 1], vel_send.at[0], vel_recv.at[0], down
        ),
        to_side(vel_buf.at[rows], vel_buf.at[0], vel_send.at[1], vel_recv.at[1], up),
    ]

    def remap(r, c):
        g = c * rows + r
        table = [
            (
                j * blocks + b,
                lambda half, j=j, b=b: received[j, b, pl.ds(half * 8, 8), :],
            )
            for j in range(nears)
            for b in range(blocks)
        ]
        his, los, weights = [], [], []
        for k in range(inters):
            at = k * groups + g
            his.append(near_ref[pl.ds(at, 1), :] * blocks + (slot_ref[pl.ds(at, 1), :] >> 7))
            los.append(slot_ref[pl.ds(at, 1), :] & 127)
            weights.append(wide(weight_ref, at))
        on_mxu = inters - ON_LANES
        picked = dot_blocks(pieces[...], his[:on_mxu], los[:on_mxu], tracers)
        if ON_LANES > 0:
            picked += pick_blocks(
                table,
                [jnp.broadcast_to(x, (8, LANES)) for x in his[on_mxu:]],
                [jnp.broadcast_to(x, (8, LANES)) for x in los[on_mxu:]],
                tracers,
            )
        sums = [jnp.zeros((8, LANES), jnp.float32)] * halves
        for weight, part in zip(weights, picked):
            sums = [sums[half] + weight * part[half] for half in range(halves)]
        return sums

    def couple(r, c, sums):
        g = c * rows + r
        mask = wide(mask_ref, g).astype(jnp.float32)
        coup = coup_ref[pl.ds(g, tracers, stride=groups), :]
        for half in range(halves):
            at = pl.ds(half * 8, 8)
            old = lev_ref[0, 2 + r, c, at, :]
            part = coup[half * 8 : half * 8 + 8]
            lev_ref[0, 2 + r, c, at, :] = old + part * mask * (sums[half] - old)

    for j in order[1:] + order[:1]:
        pack_copies[j].wait_recv()

    def split_slots(b, _):
        for j in range(nears):
            split_pieces(received[j, b], pieces, j * blocks + b, tracers)
        return 0

    lax.fori_loop(0, blocks, split_slots, 0)

    def low_rows(g, _):
        couple(g // chunks, g % chunks, remap(g // chunks, g % chunks))
        return 0

    lax.fori_loop(0, 2 * chunks, low_rows, 0, unroll=2)
    edge_copies = [
        to_side(
            lev_ref.at[0, own_low],
            lev_ref.at[0, high],
            edge_send.at[0],
            edge_recv.at[0],
            down,
        )
    ]
    for r in range(2, rows):

        def one(c, _, r=r):
            couple(r, c, remap(r, c))
            return 0

        lax.fori_loop(0, chunks, one, 0, unroll=2)
        if r >= rows - 2:
            n = r - (rows - 2)
            edge_copies.append(
                to_side(
                    lev_ref.at[0, 2 + r],
                    lev_ref.at[0, n],
                    edge_send.at[1 + n],
                    edge_recv.at[1 + n],
                    up,
                )
            )

    lane = lax.broadcasted_iota(jnp.int32, (chunks * tracers, LANES), 1)

    def stepped(field, east, west, level, vrow):
        flat = field.reshape(chunks * tracers, LANES)
        ahead = pltpu.roll(flat, LANES - 1, 1)
        behind = pltpu.roll(flat, 1, 1)
        north = jnp.where(
            lane == LANES - 1,
            jnp.concatenate([ahead[tracers:], ahead[:tracers]], axis=0),
            ahead,
        ).reshape(chunks, tracers, LANES)
        south = jnp.where(
            lane == 0,
            jnp.concatenate([behind[-tracers:], behind[:-tracers]], axis=0),
            behind,
        ).reshape(chunks, tracers, LANES)
        u = vel_buf[vrow, level]
        v = vel_buf[vrow, levels + level]
        return (
            field
            - 0.5 * u * (east - west)
            - 0.5 * v * (north - south)
            + diffusion * (east + west + north + south - 4.0 * field)
        )

    def transport(level):
        def step_one(i, _):
            first[i] = stepped(
                lev_ref[level, i + 1],
                lev_ref[level, i + 2],
                lev_ref[level, i],
                level,
                i,
            )
            return 0

        lax.fori_loop(0, rows + 2, step_one, 0, unroll=2)

        def step_two(r, _):
            value = stepped(first[r + 1], first[r + 2], first[r], level, r + 1)
            for c in range(chunks):
                out_ref[
                    pl.ds(
                        level * groups + c * rows + r, tracers, stride=levels * groups
                    ),
                    :,
                ] = value[c]
            return 0

        lax.fori_loop(0, rows, step_two, 0, unroll=2)

    for copy in side_copies:
        copy.wait()

    def inner_level(level, _):
        transport(level)
        return 0

    lax.fori_loop(1, levels, inner_level, 0)
    for copy in edge_copies:
        copy.wait()
    transport(0)
    for j in order:
        pack_copies[j].wait_send()


def split_rows(x):
    *lead, rows, width = x.shape
    chunks = width // LANES
    x = jnp.swapaxes(x.reshape(*lead, rows, chunks, LANES), -3, -2)
    return x.reshape(-1, LANES)


def per_device(
    tiles,
    tracer,
    velocity,
    coupling,
    sea_mask,
    send_rows,
    send_cols,
    intersection_near,
    intersection_slot,
    intersection_weight,
):
    _, tracers, levels, rows, width = tracer.shape
    nears, capacity = send_rows.shape[2:]
    inters = intersection_slot.shape[1]
    chunks, blocks = width // LANES, capacity // LANES
    dims = (tiles, tracers, levels, rows, chunks, nears, blocks, inters)
    dma = pltpu.SemaphoreType.DMA
    vmem = pl.BlockSpec(memory_space=pltpu.VMEM)
    f32 = jnp.float32
    out = pl.pallas_call(
        functools.partial(exchange_kernel, dims),
        out_shape=jax.ShapeDtypeStruct((tracers * levels * rows * chunks, LANES), f32),
        in_specs=[vmem] * 9,
        out_specs=vmem,
        scratch_shapes=[
            pltpu.VMEM((levels, rows + 4, chunks, tracers, LANES), f32),
            pltpu.VMEM((rows + 2, 2 * levels, chunks, 1, LANES), f32),
            pltpu.VMEM((nears, blocks, tracers, LANES), f32),
            pltpu.VMEM((nears, blocks, tracers, LANES), f32),
            pltpu.VMEM((rows + 2, chunks, tracers, LANES), f32),
            pltpu.VMEM((nears * blocks * tracers, 2 * LANES), jnp.bfloat16),
            pltpu.VMEM((rows * chunks * tracers, 2 * LANES), jnp.bfloat16),
            dma((nears,)),
            dma((nears,)),
            dma((2,)),
            dma((2,)),
            dma((3,)),
            dma((3,)),
            dma((2,)),
            dma((2,)),
        ],
        compiler_params=pltpu.CompilerParams(collective_id=0, has_side_effects=True),
    )(
        split_rows(tracer),
        split_rows(velocity),
        split_rows(coupling),
        split_rows(sea_mask),
        split_rows(send_rows),
        split_rows(send_cols),
        split_rows(intersection_near),
        split_rows(intersection_slot),
        split_rows(intersection_weight),
    )
    out = out.reshape(1, tracers, levels, chunks, rows, LANES)
    return jnp.swapaxes(out, 3, 4).reshape(tracer.shape)


def solution(mesh):
    in_specs = (
        P("comp", None, None, "tile", None),
        P("comp", None, None, "tile", None),
        P("comp", None, "tile", None),
        P("comp", "tile", None),
        P("comp", "tile", None, None),
        P("comp", "tile", None, None),
        P("comp", None, "tile", None),
        P("comp", None, "tile", None),
        P("comp", None, "tile", None),
    )
    out_specs = P("comp", None, None, "tile", None)
    return jax.shard_map(
        functools.partial(per_device, mesh.shape["tile"]),
        mesh=mesh,
        in_specs=in_specs,
        out_specs=out_specs,
        check_vma=False,
    )
```
